32 devices in a mesh: groups: 2 (over y), band: 4 (over z), img: 2 (over x), col: 2 (over core).
Axes of the slice: x: 2, y: 2, z: 4, core: 2. Of those that a mesh axis runs over, the one named last changes fastest.
Arguments:
- real_images: float32 [4, 64, 3, 128], P(('groups', 'img'), ('band', 'col')), parts along dimension 0, may hold values from -6 to 6
- tile_images: float32 [4, 64, 3, 128], P(('groups', 'img'), 'band', None, 'col'), parts along dimension 0, may hold values from -6 to 6
- rgb_weight: float32 [3, 64], replicated, may hold values from -3.5 to 3.5
- first_weight: float32 [3, 3, 64, 64], replicated, may hold values from -0.25 to 0.25
- second_weight: float32 [3, 3, 64, 128], replicated, may hold values from -0.25 to 0.25
- skip_weight: float32 [64, 128], replicated, may hold values from -0.75 to 0.75
- readout: float32 [32, 128, 64], P(('band', 'col')), may hold values from -0.01171875 to 0.01171875
Outputs:
- grad_rgb: float32 [6, 64], P('groups'), parts along dimension 0
- grad_first: float32 [6, 3, 64, 64], P('groups'), parts along dimension 0
- grad_second: float32 [6, 3, 64, 128], P('groups'), parts along dimension 0
- grad_skip: float32 [128, 128], P('groups'), parts along dimension 0
The draws below stay inside these ranges and needn't reach their ends.
There are 2 independent parts, one for each index of `groups`. The reference program is written for one: setup_inputs(seed, part) draws one part's arguments, and reference() takes and returns one part's arrays. A program takes and returns all parts, laid end to end along the dimension named above; an argument that names none is the same for every part. Nothing has to cross between parts.
All inputs are finite; a program needn't handle non-finite values.
Results may differ from the reference program's by a relative error of at most 0.00019.
Values sent between devices are 32-bit elements; how exact they have to be, the bound alone decides.
A program may use at most 64 MiB of HBM per device.

```python
import jax
import jax.numpy as jnp
from jax import lax

COLS = 128
FEAT_IN = 64
FEAT_OUT = 128
IMGS = 2
HEIGHT = 64


def level_of(rng, dims, pieces, smallest, largest):
    loudness = 1.0
    for position, parts in pieces:
        draws = jax.random.uniform(jax.random.fold_in(jax.random.fold_in(rng, 6), position), (parts,), jnp.float32, smallest / len(pieces), largest / len(pieces))
        loudness = loudness * jnp.repeat(jnp.exp(draws), dims[position] // parts).reshape((-1,) + (1,) * (len(dims) - 1 - position))
    return loudness


def gaussian(own_key, extent, scale, bound, split=(), kind=jnp.bfloat16):
    values = jax.random.normal(own_key, extent, jnp.float32) * scale
    if len(split) > 0:
        values = level_of(own_key, extent, split, -0.22, 0.18) * values
    return jnp.clip(values, min=-bound, max=bound).astype(kind)


def setup_inputs(seed: int = 0, part: int = 0) -> dict:
    key_list = jax.random.split(jax.random.key(seed), 8)
    own_keys = jax.random.split(jax.random.fold_in(key_list[7], part), 8)
    real_images = gaussian(own_keys[0], (IMGS, HEIGHT, 3, COLS), 1.0, 6.0, ((0, 2), (1, 8)), jnp.float32)
    tile_images = gaussian(own_keys[1], (IMGS, HEIGHT, 3, COLS), 1.0, 6.0, ((0, 2), (1, 4), (3, 2)), jnp.float32)
    rgb_weight = gaussian(key_list[2], (3, FEAT_IN), 3 ** -0.5, 3.5, (), jnp.float32)
    first_weight = gaussian(key_list[3], (3, 3, FEAT_IN, FEAT_IN), (9 * FEAT_IN) ** -0.5, 0.25, (), jnp.float32)
    second_weight = gaussian(key_list[4], (3, 3, FEAT_IN, FEAT_OUT), (9 * FEAT_IN) ** -0.5, 0.25, (), jnp.float32)
    skip_weight = gaussian(key_list[5], (FEAT_IN, FEAT_OUT), FEAT_IN ** -0.5, 0.75, (), jnp.float32)
    readout = gaussian(key_list[6], (HEIGHT // 2, FEAT_OUT, COLS // 2), (HEIGHT * FEAT_OUT * COLS // 4) ** -0.5, 0.01171875, ((0, 8),), jnp.float32)
    return {"real_images": real_images, "tile_images": tile_images, "rgb_weight": rgb_weight, "first_weight": first_weight, "second_weight": second_weight, "skip_weight": skip_weight, "readout": readout}


HIGHEST_PREC = lax.Precision.HIGHEST
INV_ROOT = 0.7071067811865476
GAMMA_WEIGHT = 10.0

def conv_layer(field, kernel, stride_step):
    result = lax.conv_general_dilated(field[None], kernel, (stride_step, stride_step), ((1, 1), (1, 1)), dimension_numbers=('NCHW', 'HWIO', 'NCHW'), precision=HIGHEST_PREC)
    return result[0]

def critic(image, weights, readout):
    rgb_weight, first_weight, second_weight, skip_weight = weights
    colours = jnp.transpose(image, (1, 0, 2))
    features = jax.nn.silu(jnp.einsum('chw,cd->dhw', colours, rgb_weight, precision=HIGHEST_PREC))
    hidden = jax.nn.silu(conv_layer(features, first_weight, 1))
    strided = conv_layer(hidden, second_weight, 2)
    shortcut = jnp.einsum('chw,cd->dhw', features[:, ::2, ::2], skip_weight, precision=HIGHEST_PREC)
    output = (strided + shortcut) * INV_ROOT
    return jnp.sum(jnp.transpose(readout, (1, 0, 2)) * output)

def reference(real_images, tile_images, rgb_weight, first_weight, second_weight, skip_weight, readout):

    def loss(weights):
        running = jnp.float32(0.0)
        for image_index in range(IMGS):
            real_one = real_images[image_index]
            fake_one = tile_images[image_index]
            penalty_grad = jax.grad(lambda image: critic(image, weights, readout))(real_one)
            running = running + critic(fake_one, weights, readout) - critic(real_one, weights, readout)
            running = running + 0.5 * GAMMA_WEIGHT * jnp.sum(penalty_grad * penalty_grad)
        return running
    grads = jax.grad(loss)((rgb_weight, first_weight, second_weight, skip_weight))
    return (grads[0], grads[1], grads[2], grads[3])
```

```python
import functools

import jax
import jax.numpy as jnp
from jax import lax
from jax.experimental import pallas as pl
from jax.experimental.pallas import tpu as pltpu
from jax.sharding import PartitionSpec as P

INV_ROOT = 0.7071067811865476
GAMMA_WEIGHT = 10.0
F32 = jnp.float32
BF16 = jnp.bfloat16


def halves(x):
    hi = x.astype(BF16)
    return hi, (x - hi.astype(F32)).astype(BF16)


def dot_nn(a, b):
    return lax.dot_general(a, b, (((1,), (0,)), ((), ())), preferred_element_type=F32)


def dot_nt(a, b):
    return lax.dot_general(a, b, (((1,), (1,)), ((), ())), preferred_element_type=F32)


def sigmoid(u):
    return 0.5 + 0.5 * jnp.tanh(0.5 * u)


def step_kernel(
    rows, vr, vf, ro, mask, rgbt, wf, wt, w2, sk, out,
    wfs, wts, w2s, us_h, us_l, uz_h, uz_l, zs, gh,
    fr, fr_h, fr_l, sp, s2, gp_h, gp_l, psp, ps2, hs, gf,
    df_h, df_l, ff_h, ff_l, fsp, ap_h, ap_l, gq_h, gq_l, as_h, as_l, fs, hx_h, hx_l, du,
):
    feat, wide, cols = rgbt.shape[0], ro.shape[1], vr.shape[2]
    half = cols // 2
    first, last = 4, 4 + rows

    def at(w, count=1):
        return slice(w * cols, (w + count) * cols)

    lane = lax.broadcasted_iota(jnp.int32, (feat, cols), 1)

    def right(x):
        return jnp.where(lane == 0, 0.0, pltpu.roll(x, 1, 1))

    def left(x):
        return jnp.where(lane == cols - 1, 0.0, pltpu.roll(x, cols - 1, 1))

    def split_weights(ref, dst, base, count):
        hi, lo = halves(ref[...])
        dst[base : base + ref.shape[0]] = hi
        dst[count + base : count + base + ref.shape[0]] = lo

    split_weights(wf, wfs, 0, 3 * feat)
    split_weights(wt, wts, 0, 3 * feat)
    split_weights(w2, w2s, 0, 10 * feat)
    split_weights(sk, w2s, 9 * feat, 10 * feat)

    def product(weights, count, x_hi, x_lo):
        full = weights[...]
        both = dot_nn(full, x_hi)
        return both[:count] + both[count:] + dot_nn(full[:count], x_lo)

    pick_row = lax.broadcasted_iota(jnp.int32, (half, cols), 0)
    pick_col = lax.broadcasted_iota(jnp.int32, (half, cols), 1)
    picks = [(pick_col == 2 * pick_row + (j - 1)).astype(F32).astype(BF16) for j in range(3)]
    out_rows = rows // 2
    for t in range(out_rows + 4):
        hi, lo = halves(ro[t] * INV_ROOT)
        uz_h[:, at(t)] = dot_nn(hi, picks[1]).astype(BF16)
        uz_l[:, at(t)] = dot_nn(lo, picks[1]).astype(BF16)
        if 2 <= t < 2 + out_rows:
            for j in range(3):
                us_h[j * wide : (j + 1) * wide, at(t - 2)] = dot_nn(hi, picks[j]).astype(BF16)
                us_l[j * wide : (j + 1) * wide, at(t - 2)] = dot_nn(lo, picks[j]).astype(BF16)
    for t in range(0, out_rows + 4, 2):
        zs[:, at(t, 2)] = product(w2s, 10 * feat, uz_h[:, at(t, 2)], uz_l[:, at(t, 2)])

    def tap(i, j, t):
        base = (i * 3 + j) * feat
        return zs[base : base + feat, at(t)]

    for w in range(1, last + 3):
        if w % 2 == 0:
            parts = [tap(1, j, w // 2) for j in range(3)]
        else:
            parts = [tap(2, j, (w - 1) // 2) + tap(0, j, (w + 1) // 2) for j in range(3)]
        value = parts[1] + left(parts[0]) + right(parts[2])
        gh[:, at(w)] = value * mask[w : w + 1, :]

    rgb = [rgbt[:, c : c + 1] for c in range(3)]

    def project(rows3):
        return rgb[0] * rows3[0:1, :] + rgb[1] * rows3[1:2, :] + rgb[2] * rows3[2:3, :]

    def put(hi_ref, lo_ref, w, value):
        hi, lo = halves(value)
        hi_ref[:, at(w)] = hi
        lo_ref[:, at(w)] = lo

    for w in range(last + 4):
        u = project(vr[w])
        s = sigmoid(u)
        value = u * s
        put(fr_h, fr_l, w, value)
        if first <= w < last and w % 2 == 0:
            fs[:, at((w - first) // 2)] = -value
        sp[:, at(w)] = s * (1.0 + u * (1.0 - s))
        s2[:, at(w)] = s * (1.0 - s) * (2.0 + u * (1.0 - 2.0 * s))
    for w in range(2, last + 2):
        u = project(vf[w - 2])
        s = sigmoid(u)
        value = u * s
        put(ff_h, ff_l, w, value)
        if first <= w < last and w % 2 == 0:
            fs[:, at((w - first) // 2)] += value
        fsp[:, at(w)] = s * (1.0 + u * (1.0 - s))

    def convolve(weights, hi_ref, lo_ref, w):
        x_hi = jnp.concatenate([hi_ref[:, at(w + k, 2)] for k in (-1, 0, 1)], 0)
        x_lo = jnp.concatenate([lo_ref[:, at(w + k, 2)] for k in (-1, 0, 1)], 0)
        y = product(weights, 3 * feat, x_hi, x_lo)
        return [
            (w + k, [y[j * feat : (j + 1) * feat, at(k)] for j in range(3)]) for k in range(2)
        ]

    def forward(hi_ref, lo_ref, w):
        for row, y in convolve(wfs, hi_ref, lo_ref, w):
            yield row, y[1] + right(y[0]) + left(y[2])

    def backward(hi_ref, lo_ref, w):
        for row, y in convolve(wts, hi_ref, lo_ref, w):
            yield row, y[1] + left(y[0]) + right(y[2])

    span = rows * cols

    def put_shifts(field, w, value):
        lanes = slice(field * span + (w - first) * cols, field * span + (w - first + 1) * cols)
        for j, moved in enumerate((left(value), value, right(value))):
            hi, lo = halves(moved)
            as_h[j * feat : (j + 1) * feat, lanes] = hi
            as_l[j * feat : (j + 1) * feat, lanes] = lo

    for start in range(1, last + 3, 2):
        for w, u in forward(fr_h, fr_l, start):
            s = sigmoid(u)
            prime = s * (1.0 + u * (1.0 - s))
            grad = gh[:, at(w)] * prime
            put(gp_h, gp_l, w, grad)
            if first <= w < last:
                put_shifts(2, w, GAMMA_WEIGHT * grad)
            if 3 <= w <= last:
                psp[:, at(w)] = prime
                ps2[:, at(w)] = s * (1.0 - s) * (2.0 + u * (1.0 - 2.0 * s))
                hs[:, at(w)] = -(u * s) * mask[w : w + 1, :]

    for start in range(3, last + 1, 2):
        for w, u in forward(ff_h, ff_l, start):
            s = sigmoid(u)
            grad = gh[:, at(w)] * (s * (1.0 + u * (1.0 - s)))
            put(gq_h, gq_l, w, grad)
            if first <= w < last:
                put_shifts(1, w, grad)
            hs[:, at(w)] += u * s * mask[w : w + 1, :]

    def add_skip(w, value):
        if w % 2 == 0:
            return value + zs[9 * feat : 10 * feat, at(w // 2)]
        return value

    zero = jnp.zeros((feat, cols), F32)
    acc = [zero, zero, zero]
    for start in range(2, last + 2, 2):
        for w, y in backward(gp_h, gp_l, start):
            value = add_skip(w, y)
            gu = value * sp[:, at(w)]
            keep = mask[w : w + 1, :]
            g = [jnp.sum(rgb[c] * gu, axis=0, keepdims=True) * keep for c in range(3)]
            moved = rgb[0] * g[0] + rgb[1] * g[1] + rgb[2] * g[2]
            tangent = sp[:, at(w)] * moved
            put(df_h, df_l, w, tangent)
            if first <= w < last:
                if w % 2 == 0:
                    fs[:, at((w - first) // 2)] += GAMMA_WEIGHT * tangent
                gf[:, at(w)] = GAMMA_WEIGHT * value * moved * s2[:, at(w)]
                acc = [acc[c] + (GAMMA_WEIGHT * g[c]) * gu for c in range(3)]

    for start in range(first, last, 2):
        for w, y in backward(gq_h, gq_l, start):
            gu = add_skip(w, y) * fsp[:, at(w)]
            image = vf[w - 2]
            acc = [acc[c] + image[c : c + 1, :] * gu for c in range(3)]

    for start in range(3, last + 1, 2):
        for w, dp in forward(df_h, df_l, start):
            hidden_grad = gh[:, at(w)]
            prime = psp[:, at(w)]
            total = hidden_grad * (GAMMA_WEIGHT * ps2[:, at(w)] * dp - prime)
            put(ap_h, ap_l, w, total)
            if first <= w < last:
                put_shifts(0, w, total)
            hs[:, at(w)] += GAMMA_WEIGHT * prime * dp * mask[w : w + 1, :]

    for start in range(first, last, 2):
        for w, y in backward(ap_h, ap_l, start):
            if w % 2 == 0:
                y = y - zs[9 * feat : 10 * feat, at(w // 2)]
            au = y * sp[:, at(w)] + gf[:, at(w)]
            image = vr[w]
            acc = [acc[c] + image[c : c + 1, :] * au for c in range(3)]

    for r in range(out_rows):
        for i in range(3):
            hi, lo = halves(hs[:, at(3 + 2 * r + i)])
            hx_h[i * feat : (i + 1) * feat, at(r)] = hi
            hx_l[i * feat : (i + 1) * feat, at(r)] = lo
        hi, lo = halves(fs[:, at(r)])
        hx_h[3 * feat : 4 * feat, at(r)] = hi
        hx_l[3 * feat : 4 * feat, at(r)] = lo
    second = (
        dot_nt(hx_h[...], us_h[...])
        + dot_nt(hx_l[...], us_h[...])
        + dot_nt(hx_h[...], us_l[...])
    )
    for i in range(3):
        for j in range(3):
            base = (i * 3 + j) * feat
            out[base : base + feat, :] = second[
                i * feat : (i + 1) * feat, j * wide : (j + 1) * wide
            ]
    out[9 * feat : 10 * feat, :] = second[3 * feat : 4 * feat, wide : 2 * wide]

    grad = None
    for field, (hi_ref, lo_ref) in enumerate(((fr_h, fr_l), (ff_h, ff_l), (df_h, df_l))):
        lanes = slice(field * span, (field + 1) * span)
        x_hi = jnp.concatenate([hi_ref[:, at(3 + i, rows)] for i in range(3)], 0)
        x_lo = jnp.concatenate([lo_ref[:, at(3 + i, rows)] for i in range(3)], 0)
        a_hi, a_lo = as_h[:, lanes], as_l[:, lanes]
        term = dot_nt(x_hi, a_hi) + dot_nt(x_lo, a_hi) + dot_nt(x_hi, a_lo)
        grad = term if grad is None else grad + term
    base = 10 * feat
    out[base : base + 3 * feat, :] = grad[:, : 2 * feat]
    tail = grad[:, 2 * feat :]
    base = 13 * feat
    out[base : base + feat, :] = jnp.concatenate([tail[:feat], tail[feat : 2 * feat]], 1)
    spot = lax.broadcasted_iota(jnp.int32, (feat, feat), 1)
    colour = jnp.zeros((feat, feat), F32)
    for c in range(3):
        colour = jnp.where(spot == c, jnp.sum(acc[c], axis=1, keepdims=True), colour)
    base = 14 * feat
    out[base : base + feat, :] = jnp.concatenate([tail[2 * feat :], colour], 1)


def local_step(vr, vf, ro, mask, rgb_weight, first_weight, second_weight, skip_weight):
    rows = vr.shape[0] - 8
    feat, wide = skip_weight.shape
    cols = vr.shape[2]
    wf = jnp.transpose(first_weight, (1, 3, 0, 2)).reshape(3 * feat, 3 * feat)
    wt = jnp.transpose(first_weight[::-1], (1, 2, 0, 3)).reshape(3 * feat, 3 * feat)
    w2 = second_weight.reshape(9 * feat, wide)

    def keep(height, count, kind):
        return pltpu.VMEM((height, count * cols), kind)

    def pair(height, count):
        return [keep(height, count, BF16), keep(height, count, BF16)]

    window, outs = rows + 8, rows // 2
    plain = keep(feat, window, F32)
    scratch = [
        pltpu.VMEM((6 * feat, 3 * feat), BF16),
        pltpu.VMEM((6 * feat, 3 * feat), BF16),
        pltpu.VMEM((20 * feat, wide), BF16),
        *pair(3 * wide, outs),
        *pair(wide, outs + 4),
        keep(10 * feat, outs + 4, F32),
        plain,
        plain, *pair(feat, window), plain, plain,
        *pair(feat, window), plain, plain, plain, plain,
        *pair(feat, window),
        *pair(feat, window), plain,
        *pair(feat, window), *pair(feat, window),
        *pair(3 * feat, 3 * rows),
        keep(feat, outs, F32), *pair(4 * feat, outs), plain,
    ]
    whole = pl.BlockSpec(memory_space=pltpu.VMEM)
    return pl.pallas_call(
        functools.partial(step_kernel, rows),
        out_shape=jax.ShapeDtypeStruct((15 * feat, wide), F32),
        in_specs=[whole] * 9,
        out_specs=whole,
        scratch_shapes=scratch,
        compiler_params=pltpu.CompilerParams(vmem_limit_bytes=60 * 1024 * 1024),
    )(vr, vf, ro, mask, rgb_weight.T, wf, wt, w2, skip_weight)


def neighbours(cells, above, below):
    axes = ("band", "col")
    count = lax.axis_size(axes)
    links = count - 1
    down = [(i, i + 1) for i in range(links)]
    up = [(i + 1, i) for i in range(links)]
    before = lax.ppermute(cells[cells.shape[0] - above :], axes, down)
    after = lax.ppermute(cells[:below], axes, up)
    return jnp.concatenate([before, cells, after], 0)


def unpack(total, feat):
    second = total[: 9 * feat].reshape(3, 3, feat, total.shape[1])
    skip = total[9 * feat : 10 * feat]
    pairs = total[10 * feat : 13 * feat].reshape(3, feat, 2, feat)
    low = total[13 * feat : 14 * feat]
    high = total[14 * feat : 15 * feat]
    third = jnp.stack([low[:, :feat], low[:, feat:], high[:, :feat]])
    grad_first = jnp.stack([pairs[:, :, 0], pairs[:, :, 1], third], 1)
    return high[:, feat : feat + 3].T, grad_first, second, skip


def body(real_images, tile_images, rgb_weight, first_weight, second_weight, skip_weight, readout):
    row_count = real_images.shape[1]
    axes = ("band", "col")
    total_rows = row_count * lax.axis_size(axes)
    generated = lax.all_to_all(tile_images, "col", split_axis=1, concat_axis=3, tiled=True)
    vr = neighbours(real_images[0], 4, 4)
    vf = neighbours(generated[0], 2, 2)
    ro = neighbours(readout, 2, 2)
    rows = lax.axis_index(axes) * row_count - 4 + jnp.arange(row_count + 8)
    inside = ((rows >= 0) & (rows < total_rows)).astype(F32)
    mask = jnp.broadcast_to(inside[:, None], (row_count + 8, real_images.shape[3]))
    packed = local_step(vr, vf, ro, mask, rgb_weight, first_weight, second_weight, skip_weight)
    return unpack(lax.psum(packed, ("band", "img", "col")), skip_weight.shape[0])


def solution(mesh):
    placed = (
        P(("groups", "img"), ("band", "col"), None, None),
        P(("groups", "img"), "band", None, "col"),
        P(),
        P(),
        P(),
        P(),
        P(("band", "col"), None, None),
    )
    return jax.shard_map(
        body,
        mesh=mesh,
        in_specs=placed,
        out_specs=(
            P("groups", None),
            P("groups", None, None, None),
            P("groups", None, None, None),
            P("groups", None),
        ),
        check_vma=False,
    )
```

```python
import functools

import jax
import jax.numpy as jnp
from jax import lax
from jax.experimental import pallas as pl
from jax.experimental.pallas import tpu as pltpu
from jax.sharding import PartitionSpec as P

INV_ROOT = 0.7071067811865476
GAMMA_WEIGHT = 10.0
F32 = jnp.float32
BF16 = jnp.bfloat16


def halves(x):
    hi = x.astype(BF16)
    return hi, (x - hi.astype(F32)).astype(BF16)


def dot_nn(a, b):
    return lax.dot_general(a, b, (((1,), (0,)), ((), ())), preferred_element_type=F32)


def dot_nt(a, b):
    return lax.dot_general(a, b, (((1,), (1,)), ((), ())), preferred_element_type=F32)


def sigmoid(u):
    return 0.5 + 0.5 * jnp.tanh(0.5 * u)


def step_kernel(
    rows, vr, vf, ro, mask, rgbt, wf, wt, w2, sk, out,
    wfs, wts, w2s, us_h, us_l, uz_h, uz_l, zs, gh,
    fr, fr_h, fr_l, sp, s2, gp_h, gp_l, psp, ps2, hs, gf,
    df_h, df_l, ff_h, ff_l, fsp, ap_h, ap_l, gq_h, gq_l, as_h, as_l, fs, hx_h, hx_l, du,
):
    feat, wide, cols = rgbt.shape[0], ro.shape[1], vr.shape[2]
    half = cols // 2
    first, last = 4, 4 + rows

    def at(w, count=1):
        return slice(w * cols, (w + count) * cols)

    lane = lax.broadcasted_iota(jnp.int32, (feat, cols), 1)

    def right(x):
        return jnp.where(lane == 0, 0.0, pltpu.roll(x, 1, 1))

    def left(x):
        return jnp.where(lane == cols - 1, 0.0, pltpu.roll(x, cols - 1, 1))

    def split_weights(ref, dst, base, count):
        hi, lo = halves(ref[...])
        dst[base : base + ref.shape[0]] = hi
        dst[count + base : count + base + ref.shape[0]] = lo

    split_weights(wf, wfs, 0, 3 * feat)
    split_weights(wt, wts, 0, 3 * feat)
    split_weights(w2, w2s, 0, 10 * feat)
    split_weights(sk, w2s, 9 * feat, 10 * feat)

    def product(weights, count, x_hi, x_lo):
        full = weights[...]
        both = dot_nn(full, x_hi)
        return both[:count] + both[count:] + dot_nn(full[:count], x_lo)

    pick_row = lax.broadcasted_iota(jnp.int32, (half, cols), 0)
    pick_col = lax.broadcasted_iota(jnp.int32, (half, cols), 1)
    picks = [(pick_col == 2 * pick_row + (j - 1)).astype(F32).astype(BF16) for j in range(3)]
    out_rows = rows // 2
    for t in range(out_rows + 4):
        hi, lo = halves(ro[t] * INV_ROOT)
        uz_h[:, at(t)] = dot_nn(hi, picks[1]).astype(BF16)
        uz_l[:, at(t)] = dot_nn(lo, picks[1]).astype(BF16)
        if 2 <= t < 2 + out_rows:
            for j in range(3):
                us_h[j * wide : (j + 1) * wide, at(t - 2)] = dot_nn(hi, picks[j]).astype(BF16)
                us_l[j * wide : (j + 1) * wide, at(t - 2)] = dot_nn(lo, picks[j]).astype(BF16)
    for t in range(0, out_rows + 4, 2):
        zs[:, at(t, 2)] = product(w2s, 10 * feat, uz_h[:, at(t, 2)], uz_l[:, at(t, 2)])

    def tap(i, j, t):
        base = (i * 3 + j) * feat
        return zs[base : base + feat, at(t)]

    for w in range(1, last + 3):
        if w % 2 == 0:
            parts = [tap(1, j, w // 2) for j in range(3)]
        else:
            parts = [tap(2, j, (w - 1) // 2) + tap(0, j, (w + 1) // 2) for j in range(3)]
        value = parts[1] + left(parts[0]) + right(parts[2])
        gh[:, at(w)] = value * mask[w : w + 1, :]

    rgb = [rgbt[:, c : c + 1] for c in range(3)]

    def project(rows3):
        return rgb[0] * rows3[0:1, :] + rgb[1] * rows3[1:2, :] + rgb[2] * rows3[2:3, :]

    def put(hi_ref, lo_ref, w, value):
        hi, lo = halves(value)
        hi_ref[:, at(w)] = hi
        lo_ref[:, at(w)] = lo

    for w in range(last + 4):
        u = project(vr[w])
        s = sigmoid(u)
        value = u * s
        put(fr_h, fr_l, w, value)
        if first <= w < last and w % 2 == 0:
            fs[:, at((w - first) // 2)] = -value
        sp[:, at(w)] = s * (1.0 + u * (1.0 - s))
        s2[:, at(w)] = s * (1.0 - s) * (2.0 + u * (1.0 - 2.0 * s))
    for w in range(2, last + 2):
        u = project(vf[w - 2])
        s = sigmoid(u)
        value = u * s
        put(ff_h, ff_l, w, value)
        if first <= w < last and w % 2 == 0:
            fs[:, at((w - first) // 2)] += value
        fsp[:, at(w)] = s * (1.0 + u * (1.0 - s))

    def convolve(weights, hi_ref, lo_ref, w):
        x_hi = jnp.concatenate([hi_ref[:, at(w + k, 2)] for k in (-1, 0, 1)], 0)
        x_lo = jnp.concatenate([lo_ref[:, at(w + k, 2)] for k in (-1, 0, 1)], 0)
        y = product(weights, 3 * feat, x_hi, x_lo)
        return [
            (w + k, [y[j * feat : (j + 1) * feat, at(k)] for j in range(3)]) for k in range(2)
        ]

    def forward(hi_ref, lo_ref, w):
        for row, y in convolve(wfs, hi_ref, lo_ref, w):
            yield row, y[1] + right(y[0]) + left(y[2])

    def backward(hi_ref, lo_ref, w):
        for row, y in convolve(wts, hi_ref, lo_ref, w):
            yield row, y[1] + left(y[0]) + right(y[2])

    span = rows * cols

    def put_shifts(field, w, value):
        lanes = slice(field * span + (w - first) * cols, field * span + (w - first + 1) * cols)
        for j, moved in enumerate((left(value), value, right(value))):
            hi, lo = halves(moved)
            as_h[j * feat : (j + 1) * feat, lanes] = hi
            as_l[j * feat : (j + 1) * feat, lanes] = lo

    for start in range(1, last + 3, 2):
        for w, u in forward(fr_h, fr_l, start):
            s = sigmoid(u)
            prime = s * (1.0 + u * (1.0 - s))
            grad = gh[:, at(w)] * prime
            put(gp_h, gp_l, w, grad)
            if first <= w < last:
                put_shifts(2, w, GAMMA_WEIGHT * grad)
            if 3 <= w <= last:
                psp[:, at(w)] = prime
                ps2[:, at(w)] = s * (1.0 - s) * (2.0 + u * (1.0 - 2.0 * s))
                hs[:, at(w)] = -(u * s) * mask[w : w + 1, :]

    for start in range(3, last + 1, 2):
        for w, u in forward(ff_h, ff_l, start):
            s = sigmoid(u)
            grad = gh[:, at(w)] * (s * (1.0 + u * (1.0 - s)))
            put(gq_h, gq_l, w, grad)
            if first <= w < last:
                put_shifts(1, w, grad)
            hs[:, at(w)] += u * s * mask[w : w + 1, :]

    def add_skip(w, value):
        if w % 2 == 0:
            return value + zs[9 * feat : 10 * feat, at(w // 2)]
        return value

    zero = jnp.zeros((feat, cols), F32)
    acc = [zero, zero, zero]
    for start in range(2, last + 2, 2):
        for w, y in backward(gp_h, gp_l, start):
            value = add_skip(w, y)
            gu = value * sp[:, at(w)]
            keep = mask[w : w + 1, :]
            g = [jnp.sum(rgb[c] * gu, axis=0, keepdims=True) * keep for c in range(3)]
            moved = rgb[0] * g[0] + rgb[1] * g[1] + rgb[2] * g[2]
            tangent = sp[:, at(w)] * moved
            put(df_h, df_l, w, tangent)
            if first <= w < last:
                if w % 2 == 0:
                    fs[:, at((w - first) // 2)] += GAMMA_WEIGHT * tangent
                gf[:, at(w)] = GAMMA_WEIGHT * value * moved * s2[:, at(w)]
                acc = [acc[c] + (GAMMA_WEIGHT * g[c]) * gu for c in range(3)]

    for start in range(first, last, 2):
        for w, y in backward(gq_h, gq_l, start):
            gu = add_skip(w, y) * fsp[:, at(w)]
            image = vf[w - 2]
            acc = [acc[c] + image[c : c + 1, :] * gu for c in range(3)]

    for start in range(3, last + 1, 2):
        for w, dp in forward(df_h, df_l, start):
            hidden_grad = gh[:, at(w)]
            prime = psp[:, at(w)]
            total = hidden_grad * (GAMMA_WEIGHT * ps2[:, at(w)] * dp - prime)
            put(ap_h, ap_l, w, total)
            if first <= w < last:
                put_shifts(0, w, total)
            hs[:, at(w)] += GAMMA_WEIGHT * prime * dp * mask[w : w + 1, :]

    for start in range(first, last, 2):
        for w, y in backward(ap_h, ap_l, start):
            if w % 2 == 0:
                y = y - zs[9 * feat : 10 * feat, at(w // 2)]
            au = y * sp[:, at(w)] + gf[:, at(w)]
            image = vr[w]
            acc = [acc[c] + image[c : c + 1, :] * au for c in range(3)]

    for r in range(out_rows):
        for i in range(3):
            hi, lo = halves(hs[:, at(3 + 2 * r + i)])
            hx_h[i * feat : (i + 1) * feat, at(r)] = hi
            hx_l[i * feat : (i + 1) * feat, at(r)] = lo
        hi, lo = halves(fs[:, at(r)])
        hx_h[3 * feat : 4 * feat, at(r)] = hi
        hx_l[3 * feat : 4 * feat, at(r)] = lo
    second = (
        dot_nt(hx_h[...], us_h[...])
        + dot_nt(hx_l[...], us_h[...])
        + dot_nt(hx_h[...], us_l[...])
    )
    for i in range(3):
        for j in range(3):
            base = (i * 3 + j) * feat
            out[base : base + feat, :] = second[
                i * feat : (i + 1) * feat, j * wide : (j + 1) * wide
            ]
    out[9 * feat : 10 * feat, :] = second[3 * feat : 4 * feat, wide : 2 * wide]

    grad = None
    for field, (hi_ref, lo_ref) in enumerate(((fr_h, fr_l), (ff_h, ff_l), (df_h, df_l))):
        lanes = slice(field * span, (field + 1) * span)
        x_hi = jnp.concatenate([hi_ref[:, at(3 + i, rows)] for i in range(3)], 0)
        x_lo = jnp.concatenate([lo_ref[:, at(3 + i, rows)] for i in range(3)], 0)
        a_hi, a_lo = as_h[:, lanes], as_l[:, lanes]
        term = dot_nt(x_hi, a_hi) + dot_nt(x_lo, a_hi) + dot_nt(x_hi, a_lo)
        grad = term if grad is None else grad + term
    base = 10 * feat
    out[base : base + 3 * feat, :] = grad[:, : 2 * feat]
    tail = grad[:, 2 * feat :]
    base = 13 * feat
    out[base : base + feat, :] = jnp.concatenate([tail[:feat], tail[feat : 2 * feat]], 1)
    spot = lax.broadcasted_iota(jnp.int32, (feat, feat), 1)
    colour = jnp.zeros((feat, feat), F32)
    for c in range(3):
        colour = jnp.where(spot == c, jnp.sum(acc[c], axis=1, keepdims=True), colour)
    base = 14 * feat
    out[base : base + feat, :] = jnp.concatenate([tail[2 * feat :], colour], 1)
    if out.shape[0] > 15 * feat:
        out[15 * feat :, :] = jnp.zeros((out.shape[0] - 15 * feat, wide), F32)


REDUCE_AXES = ("col", "img", "band")


def reduce_kernel(sizes, x, out, *scratch):
    count = len(sizes)
    arrive, sums = scratch[:count], scratch[count : 2 * count - 1]
    send_in, recv_in = scratch[2 * count - 1 : 3 * count - 1], scratch[3 * count - 1 : 4 * count - 1]
    send_out, recv_out = scratch[4 * count - 1 : 5 * count - 1], scratch[5 * count - 1 :]
    places = [lax.axis_index(name) for name in REDUCE_AXES]

    barrier = pltpu.get_barrier_semaphore()
    for k, name in enumerate(REDUCE_AXES):
        for d in range(1, sizes[k]):
            pl.semaphore_signal(
                barrier,
                inc=1,
                device_id={name: lax.rem(places[k] + d, sizes[k])},
                device_id_type=pl.DeviceIdType.MESH,
            )
    pl.semaphore_wait(barrier, sum(sizes) - count)

    held, offset, height = x, 0, x.shape[0]
    spans = []
    for k, name in enumerate(REDUCE_AXES):
        spans.append((offset, height))
        height = height // sizes[k]
        copies = []
        for d in range(1, sizes[k]):
            peer = lax.rem(places[k] + d, sizes[k])
            copies.append(
                pltpu.make_async_remote_copy(
                    src_ref=held.at[pl.ds(pl.multiple_of(peer * height, 8), height)],
                    dst_ref=arrive[k].at[d - 1],
                    send_sem=send_in[k].at[d - 1],
                    recv_sem=recv_in[k].at[d - 1],
                    device_id={name: peer},
                    device_id_type=pl.DeviceIdType.MESH,
                )
            )
        for copy in copies:
            copy.start()
        for copy in copies:
            copy.wait()
        total = held[pl.ds(pl.multiple_of(places[k] * height, 8), height), :]
        for d in range(1, sizes[k]):
            total = total + arrive[k][d - 1]
        offset = offset + places[k] * height
        if k < count - 1:
            sums[k][...] = total
            held = sums[k]
        else:
            out[pl.ds(pl.multiple_of(offset, 8), height), :] = total

    for k in reversed(range(count)):
        name = REDUCE_AXES[k]
        height = spans[k][1] // sizes[k]
        own = pl.ds(pl.multiple_of(spans[k][0] + places[k] * height, 8), height)
        copies = []
        for d in range(1, sizes[k]):
            copies.append(
                pltpu.make_async_remote_copy(
                    src_ref=out.at[own],
                    dst_ref=out.at[own],
                    send_sem=send_out[k].at[d - 1],
                    recv_sem=recv_out[k].at[d - 1],
                    device_id={name: lax.rem(places[k] + d, sizes[k])},
                    device_id_type=pl.DeviceIdType.MESH,
                )
            )
        for copy in copies:
            copy.start()
        for copy in copies:
            copy.wait()


def reduce_all(packed):
    sizes = [lax.axis_size(name) for name in REDUCE_AXES]
    height, width = packed.shape
    arrive, sums = [], []
    for k, size in enumerate(sizes):
        height = height // size
        arrive.append(pltpu.VMEM((size - 1, height, width), F32))
        if k < len(sizes) - 1:
            sums.append(pltpu.VMEM((height, width), F32))
    waits = [pltpu.SemaphoreType.DMA((size - 1,)) for size in sizes]
    whole = pl.BlockSpec(memory_space=pltpu.VMEM)
    return pl.pallas_call(
        functools.partial(reduce_kernel, sizes),
        out_shape=jax.ShapeDtypeStruct(packed.shape, F32),
        in_specs=[whole],
        out_specs=whole,
        scratch_shapes=[*arrive, *sums, *waits, *waits, *waits, *waits],
        compiler_params=pltpu.CompilerParams(collective_id=0, has_side_effects=True),
    )(packed)


def local_step(vr, vf, ro, mask, rgb_weight, first_weight, second_weight, skip_weight):
    rows = vr.shape[0] - 8
    feat, wide = skip_weight.shape
    cols = vr.shape[2]
    wf = jnp.transpose(first_weight, (1, 3, 0, 2)).reshape(3 * feat, 3 * feat)
    wt = jnp.transpose(first_weight[::-1], (1, 2, 0, 3)).reshape(3 * feat, 3 * feat)
    w2 = second_weight.reshape(9 * feat, wide)

    def keep(height, count, kind):
        return pltpu.VMEM((height, count * cols), kind)

    def pair(height, count):
        return [keep(height, count, BF16), keep(height, count, BF16)]

    window, outs = rows + 8, rows // 2
    plain = keep(feat, window, F32)
    scratch = [
        pltpu.VMEM((6 * feat, 3 * feat), BF16),
        pltpu.VMEM((6 * feat, 3 * feat), BF16),
        pltpu.VMEM((20 * feat, wide), BF16),
        *pair(3 * wide, outs),
        *pair(wide, outs + 4),
        keep(10 * feat, outs + 4, F32),
        plain,
        plain, *pair(feat, window), plain, plain,
        *pair(feat, window), plain, plain, plain, plain,
        *pair(feat, window),
        *pair(feat, window), plain,
        *pair(feat, window), *pair(feat, window),
        *pair(3 * feat, 3 * rows),
        keep(feat, outs, F32), *pair(4 * feat, outs), plain,
    ]
    whole = pl.BlockSpec(memory_space=pltpu.VMEM)
    grain = 8 * lax.axis_size(REDUCE_AXES)
    return pl.pallas_call(
        functools.partial(step_kernel, rows),
        out_shape=jax.ShapeDtypeStruct((-(-15 * feat // grain) * grain, wide), F32),
        in_specs=[whole] * 9,
        out_specs=whole,
        scratch_shapes=scratch,
        compiler_params=pltpu.CompilerParams(vmem_limit_bytes=60 * 1024 * 1024),
    )(vr, vf, ro, mask, rgb_weight.T, wf, wt, w2, skip_weight)


def neighbours(cells, above, below):
    axes = ("band", "col")
    count = lax.axis_size(axes)
    links = count - 1
    down = [(i, i + 1) for i in range(links)]
    up = [(i + 1, i) for i in range(links)]
    before = lax.ppermute(cells[cells.shape[0] - above :], axes, down)
    after = lax.ppermute(cells[:below], axes, up)
    return jnp.concatenate([before, cells, after], 0)


def unpack(total, feat):
    second = total[: 9 * feat].reshape(3, 3, feat, total.shape[1])
    skip = total[9 * feat : 10 * feat]
    pairs = total[10 * feat : 13 * feat].reshape(3, feat, 2, feat)
    low = total[13 * feat : 14 * feat]
    high = total[14 * feat : 15 * feat]
    third = jnp.stack([low[:, :feat], low[:, feat:], high[:, :feat]])
    grad_first = jnp.stack([pairs[:, :, 0], pairs[:, :, 1], third], 1)
    return high[:, feat : feat + 3].T, grad_first, second, skip


def body(real_images, tile_images, rgb_weight, first_weight, second_weight, skip_weight, readout):
    row_count = real_images.shape[1]
    axes = ("band", "col")
    total_rows = row_count * lax.axis_size(axes)
    generated = lax.all_to_all(tile_images, "col", split_axis=1, concat_axis=3, tiled=True)
    vr = neighbours(real_images[0], 4, 4)
    vf = neighbours(generated[0], 2, 2)
    ro = neighbours(readout, 2, 2)
    rows = lax.axis_index(axes) * row_count - 4 + jnp.arange(row_count + 8)
    inside = ((rows >= 0) & (rows < total_rows)).astype(F32)
    mask = jnp.broadcast_to(inside[:, None], (row_count + 8, real_images.shape[3]))
    packed = local_step(vr, vf, ro, mask, rgb_weight, first_weight, second_weight, skip_weight)
    return unpack(reduce_all(packed), skip_weight.shape[0])


def solution(mesh):
    placed = (
        P(("groups", "img"), ("band", "col"), None, None),
        P(("groups", "img"), "band", None, "col"),
        P(),
        P(),
        P(),
        P(),
        P(("band", "col"), None, None),
    )
    return jax.shard_map(
        body,
        mesh=mesh,
        in_specs=placed,
        out_specs=(
            P("groups", None),
            P("groups", None, None, None),
            P("groups", None, None, None),
            P("groups", None),
        ),
        check_vma=False,
    )
```

```python
import functools

import jax
import jax.numpy as jnp
from jax import lax
from jax.experimental import pallas as pl
from jax.experimental.pallas import tpu as pltpu
from jax.sharding import PartitionSpec as P

INV_ROOT = 0.7071067811865476
GAMMA_WEIGHT = 10.0
F32 = jnp.float32
BF16 = jnp.bfloat16


def halves(x):
    hi = x.astype(BF16)
    return hi, (x - hi.astype(F32)).astype(BF16)


def dot_nn(a, b):
    return lax.dot_general(a, b, (((1,), (0,)), ((), ())), preferred_element_type=F32)


def dot_nt(a, b):
    return lax.dot_general(a, b, (((1,), (1,)), ((), ())), preferred_element_type=F32)


def sigmoid(u):
    return 0.5 + 0.5 * jnp.tanh(0.5 * u)


def step_kernel(
    rows, vr, vf, ro, mask, rgbt, wf, wt, w2, sk, out,
    wfs, wts, w2s, us_h, us_l, uz_h, uz_l, zs, gh,
    fr, fr_h, fr_l, sp, s2, gp_h, gp_l, psp, ps2, hs, gf,
    df_h, df_l, ff_h, ff_l, fsp, ap_h, ap_l, gq_h, gq_l, as_h, as_l, fs, hx_h, hx_l, du,
):
    feat, wide, cols = rgbt.shape[0], ro.shape[1], vr.shape[2]
    half = cols // 2
    first, last = 4, 4 + rows

    def at(w, count=1):
        return slice(w * cols, (w + count) * cols)

    lane = lax.broadcasted_iota(jnp.int32, (feat, cols), 1)

    def right(x):
        return jnp.where(lane == 0, 0.0, pltpu.roll(x, 1, 1))

    def left(x):
        return jnp.where(lane == cols - 1, 0.0, pltpu.roll(x, cols - 1, 1))

    def split_weights(ref, dst, base, count):
        hi, lo = halves(ref[...])
        dst[base : base + ref.shape[0]] = hi
        dst[count + base : count + base + ref.shape[0]] = lo

    split_weights(wf, wfs, 0, 3 * feat)
    split_weights(wt, wts, 0, 3 * feat)
    split_weights(w2, w2s, 0, 10 * feat)
    split_weights(sk, w2s, 9 * feat, 10 * feat)

    def product(weights, count, x_hi, x_lo):
        full = weights[...]
        both = dot_nn(full, x_hi)
        return both[:count] + both[count:] + dot_nn(full[:count], x_lo)

    pick_row = lax.broadcasted_iota(jnp.int32, (half, cols), 0)
    pick_col = lax.broadcasted_iota(jnp.int32, (half, cols), 1)
    picks = [(pick_col == 2 * pick_row + (j - 1)).astype(F32).astype(BF16) for j in range(3)]
    out_rows = rows // 2
    for t in range(out_rows + 4):
        hi, lo = halves(ro[t] * (INV_ROOT * mask[2 * t : 2 * t + 1, :half]))
        uz_h[:, at(t)] = dot_nn(hi, picks[1]).astype(BF16)
        uz_l[:, at(t)] = dot_nn(lo, picks[1]).astype(BF16)
        if 2 <= t < 2 + out_rows:
            for j in range(3):
                us_h[j * wide : (j + 1) * wide, at(t - 2)] = dot_nn(hi, picks[j]).astype(BF16)
                us_l[j * wide : (j + 1) * wide, at(t - 2)] = dot_nn(lo, picks[j]).astype(BF16)
    for t in range(0, out_rows + 4, 2):
        zs[:, at(t, 2)] = product(w2s, 10 * feat, uz_h[:, at(t, 2)], uz_l[:, at(t, 2)])

    def tap(i, j, t):
        base = (i * 3 + j) * feat
        return zs[base : base + feat, at(t)]

    for w in range(1, last + 3):
        if w % 2 == 0:
            parts = [tap(1, j, w // 2) for j in range(3)]
        else:
            parts = [tap(2, j, (w - 1) // 2) + tap(0, j, (w + 1) // 2) for j in range(3)]
        value = parts[1] + left(parts[0]) + right(parts[2])
        gh[:, at(w)] = value * mask[w : w + 1, :]

    rgb = [rgbt[:, c : c + 1] for c in range(3)]

    def project(rows3):
        return rgb[0] * rows3[0:1, :] + rgb[1] * rows3[1:2, :] + rgb[2] * rows3[2:3, :]

    def put(hi_ref, lo_ref, w, value):
        hi, lo = halves(value)
        hi_ref[:, at(w)] = hi
        lo_ref[:, at(w)] = lo

    for w in range(last + 4):
        u = project(vr[w] * mask[w : w + 1, :])
        s = sigmoid(u)
        value = u * s
        put(fr_h, fr_l, w, value)
        if first <= w < last and w % 2 == 0:
            fs[:, at((w - first) // 2)] = -value
        sp[:, at(w)] = s * (1.0 + u * (1.0 - s))
        s2[:, at(w)] = s * (1.0 - s) * (2.0 + u * (1.0 - 2.0 * s))
    for w in range(2, last + 2):
        u = project(vf[w - 2] * mask[w : w + 1, :])
        s = sigmoid(u)
        value = u * s
        put(ff_h, ff_l, w, value)
        if first <= w < last and w % 2 == 0:
            fs[:, at((w - first) // 2)] += value
        fsp[:, at(w)] = s * (1.0 + u * (1.0 - s))

    def convolve(weights, hi_ref, lo_ref, w):
        x_hi = jnp.concatenate([hi_ref[:, at(w + k, 2)] for k in (-1, 0, 1)], 0)
        x_lo = jnp.concatenate([lo_ref[:, at(w + k, 2)] for k in (-1, 0, 1)], 0)
        y = product(weights, 3 * feat, x_hi, x_lo)
        return [
            (w + k, [y[j * feat : (j + 1) * feat, at(k)] for j in range(3)]) for k in range(2)
        ]

    def forward(hi_ref, lo_ref, w):
        for row, y in convolve(wfs, hi_ref, lo_ref, w):
            yield row, y[1] + right(y[0]) + left(y[2])

    def backward(hi_ref, lo_ref, w):
        for row, y in convolve(wts, hi_ref, lo_ref, w):
            yield row, y[1] + left(y[0]) + right(y[2])

    span = rows * cols

    def put_shifts(field, w, value):
        lanes = slice(field * span + (w - first) * cols, field * span + (w - first + 1) * cols)
        for j, moved in enumerate((left(value), value, right(value))):
            hi, lo = halves(moved)
            as_h[j * feat : (j + 1) * feat, lanes] = hi
            as_l[j * feat : (j + 1) * feat, lanes] = lo

    for start in range(1, last + 3, 2):
        for w, u in forward(fr_h, fr_l, start):
            s = sigmoid(u)
            prime = s * (1.0 + u * (1.0 - s))
            grad = gh[:, at(w)] * prime
            put(gp_h, gp_l, w, grad)
            if first <= w < last:
                put_shifts(2, w, GAMMA_WEIGHT * grad)
            if 3 <= w <= last:
                psp[:, at(w)] = prime
                ps2[:, at(w)] = s * (1.0 - s) * (2.0 + u * (1.0 - 2.0 * s))
                hs[:, at(w)] = -(u * s) * mask[w : w + 1, :]

    for start in range(3, last + 1, 2):
        for w, u in forward(ff_h, ff_l, start):
            s = sigmoid(u)
            grad = gh[:, at(w)] * (s * (1.0 + u * (1.0 - s)))
            put(gq_h, gq_l, w, grad)
            if first <= w < last:
                put_shifts(1, w, grad)
            hs[:, at(w)] += u * s * mask[w : w + 1, :]

    def add_skip(w, value):
        if w % 2 == 0:
            return value + zs[9 * feat : 10 * feat, at(w // 2)]
        return value

    zero = jnp.zeros((feat, cols), F32)
    acc = [zero, zero, zero]
    for start in range(2, last + 2, 2):
        for w, y in backward(gp_h, gp_l, start):
            value = add_skip(w, y)
            gu = value * sp[:, at(w)]
            keep = mask[w : w + 1, :]
            g = [jnp.sum(rgb[c] * gu, axis=0, keepdims=True) * keep for c in range(3)]
            moved = rgb[0] * g[0] + rgb[1] * g[1] + rgb[2] * g[2]
            tangent = sp[:, at(w)] * moved
            put(df_h, df_l, w, tangent)
            if first <= w < last:
                if w % 2 == 0:
                    fs[:, at((w - first) // 2)] += GAMMA_WEIGHT * tangent
                gf[:, at(w)] = GAMMA_WEIGHT * value * moved * s2[:, at(w)]
                acc = [acc[c] + (GAMMA_WEIGHT * g[c]) * gu for c in range(3)]

    for start in range(first, last, 2):
        for w, y in backward(gq_h, gq_l, start):
            gu = add_skip(w, y) * fsp[:, at(w)]
            image = vf[w - 2]
            acc = [acc[c] + image[c : c + 1, :] * gu for c in range(3)]

    for start in range(3, last + 1, 2):
        for w, dp in forward(df_h, df_l, start):
            hidden_grad = gh[:, at(w)]
            prime = psp[:, at(w)]
            total = hidden_grad * (GAMMA_WEIGHT * ps2[:, at(w)] * dp - prime)
            put(ap_h, ap_l, w, total)
            if first <= w < last:
                put_shifts(0, w, total)
            hs[:, at(w)] += GAMMA_WEIGHT * prime * dp * mask[w : w + 1, :]

    for start in range(first, last, 2):
        for w, y in backward(ap_h, ap_l, start):
            if w % 2 == 0:
                y = y - zs[9 * feat : 10 * feat, at(w // 2)]
            au = y * sp[:, at(w)] + gf[:, at(w)]
            image = vr[w]
            acc = [acc[c] + image[c : c + 1, :] * au for c in range(3)]

    for r in range(out_rows):
        for i in range(3):
            hi, lo = halves(hs[:, at(3 + 2 * r + i)])
            hx_h[i * feat : (i + 1) * feat, at(r)] = hi
            hx_l[i * feat : (i + 1) * feat, at(r)] = lo
        hi, lo = halves(fs[:, at(r)])
        hx_h[3 * feat : 4 * feat, at(r)] = hi
        hx_l[3 * feat : 4 * feat, at(r)] = lo
    second = (
        dot_nt(hx_h[...], us_h[...])
        + dot_nt(hx_l[...], us_h[...])
        + dot_nt(hx_h[...], us_l[...])
    )
    for i in range(3):
        for j in range(3):
            base = (i * 3 + j) * feat
            out[base : base + feat, :] = second[
                i * feat : (i + 1) * feat, j * wide : (j + 1) * wide
            ]
    out[9 * feat : 10 * feat, :] = second[3 * feat : 4 * feat, wide : 2 * wide]

    grad = None
    for field, (hi_ref, lo_ref) in enumerate(((fr_h, fr_l), (ff_h, ff_l), (df_h, df_l))):
        lanes = slice(field * span, (field + 1) * span)
        x_hi = jnp.concatenate([hi_ref[:, at(3 + i, rows)] for i in range(3)], 0)
        x_lo = jnp.concatenate([lo_ref[:, at(3 + i, rows)] for i in range(3)], 0)
        a_hi, a_lo = as_h[:, lanes], as_l[:, lanes]
        term = dot_nt(x_hi, a_hi) + dot_nt(x_lo, a_hi) + dot_nt(x_hi, a_lo)
        grad = term if grad is None else grad + term
    base = 10 * feat
    out[base : base + 3 * feat, :] = grad[:, : 2 * feat]
    tail = grad[:, 2 * feat :]
    base = 13 * feat
    out[base : base + feat, :] = jnp.concatenate([tail[:feat], tail[feat : 2 * feat]], 1)
    spot = lax.broadcasted_iota(jnp.int32, (feat, feat), 1)
    colour = jnp.zeros((feat, feat), F32)
    for c in range(3):
        colour = jnp.where(spot == c, jnp.sum(acc[c], axis=1, keepdims=True), colour)
    base = 14 * feat
    out[base : base + feat, :] = jnp.concatenate([tail[2 * feat :], colour], 1)
    if out.shape[0] > 15 * feat:
        out[15 * feat :, :] = jnp.zeros((out.shape[0] - 15 * feat, wide), F32)


REDUCE_AXES = ("col", "img", "band")


def reduce_kernel(sizes, x, out, *scratch):
    count = len(sizes)
    arrive, sums = scratch[:count], scratch[count : 2 * count - 1]
    send_in, recv_in = scratch[2 * count - 1 : 3 * count - 1], scratch[3 * count - 1 : 4 * count - 1]
    send_out, recv_out = scratch[4 * count - 1 : 5 * count - 1], scratch[5 * count - 1 :]
    places = [lax.axis_index(name) for name in REDUCE_AXES]

    barrier = pltpu.get_barrier_semaphore()
    for k, name in enumerate(REDUCE_AXES):
        for d in range(1, sizes[k]):
            pl.semaphore_signal(
                barrier,
                inc=1,
                device_id={name: lax.rem(places[k] + d, sizes[k])},
                device_id_type=pl.DeviceIdType.MESH,
            )
    pl.semaphore_wait(barrier, sum(sizes) - count)

    held, offset, height = x, 0, x.shape[0]
    spans = []
    for k, name in enumerate(REDUCE_AXES):
        spans.append((offset, height))
        height = height // sizes[k]
        copies = []
        for d in range(1, sizes[k]):
            peer = lax.rem(places[k] + d, sizes[k])
            copies.append(
                pltpu.make_async_remote_copy(
                    src_ref=held.at[pl.ds(pl.multiple_of(peer * height, 8), height)],
                    dst_ref=arrive[k].at[d - 1],
                    send_sem=send_in[k].at[d - 1],
                    recv_sem=recv_in[k].at[d - 1],
                    device_id={name: peer},
                    device_id_type=pl.DeviceIdType.MESH,
                )
            )
        for copy in copies:
            copy.start()
        for copy in copies:
            copy.wait()
        total = held[pl.ds(pl.multiple_of(places[k] * height, 8), height), :]
        for d in range(1, sizes[k]):
            total = total + arrive[k][d - 1]
        offset = offset + places[k] * height
        if k < count - 1:
            sums[k][...] = total
            held = sums[k]
        else:
            out[pl.ds(pl.multiple_of(offset, 8), height), :] = total

    for k in reversed(range(count)):
        name = REDUCE_AXES[k]
        height = spans[k][1] // sizes[k]
        own = pl.ds(pl.multiple_of(spans[k][0] + places[k] * height, 8), height)
        copies = []
        for d in range(1, sizes[k]):
            copies.append(
                pltpu.make_async_remote_copy(
                    src_ref=out.at[own],
                    dst_ref=out.at[own],
                    send_sem=send_out[k].at[d - 1],
                    recv_sem=recv_out[k].at[d - 1],
                    device_id={name: lax.rem(places[k] + d, sizes[k])},
                    device_id_type=pl.DeviceIdType.MESH,
                )
            )
        for copy in copies:
            copy.start()
        for copy in copies:
            copy.wait()


def reduce_all(packed):
    sizes = [lax.axis_size(name) for name in REDUCE_AXES]
    height, width = packed.shape
    arrive, sums = [], []
    for k, size in enumerate(sizes):
        height = height // size
        arrive.append(pltpu.VMEM((size - 1, height, width), F32))
        if k < len(sizes) - 1:
            sums.append(pltpu.VMEM((height, width), F32))
    waits = [pltpu.SemaphoreType.DMA((size - 1,)) for size in sizes]
    whole = pl.BlockSpec(memory_space=pltpu.VMEM)
    return pl.pallas_call(
        functools.partial(reduce_kernel, sizes),
        out_shape=jax.ShapeDtypeStruct(packed.shape, F32),
        in_specs=[whole],
        out_specs=whole,
        scratch_shapes=[*arrive, *sums, *waits, *waits, *waits, *waits],
        compiler_params=pltpu.CompilerParams(collective_id=0, has_side_effects=True),
    )(packed)


def local_step(vr, vf, ro, mask, rgb_weight, first_weight, second_weight, skip_weight):
    rows = vr.shape[0] - 8
    feat, wide = skip_weight.shape
    cols = vr.shape[2]
    wf = jnp.transpose(first_weight, (1, 3, 0, 2)).reshape(3 * feat, 3 * feat)
    wt = jnp.transpose(first_weight[::-1], (1, 2, 0, 3)).reshape(3 * feat, 3 * feat)
    w2 = second_weight.reshape(9 * feat, wide)

    def keep(height, count, kind):
        return pltpu.VMEM((height, count * cols), kind)

    def pair(height, count):
        return [keep(height, count, BF16), keep(height, count, BF16)]

    window, outs = rows + 8, rows // 2
    plain = keep(feat, window, F32)
    scratch = [
        pltpu.VMEM((6 * feat, 3 * feat), BF16),
        pltpu.VMEM((6 * feat, 3 * feat), BF16),
        pltpu.VMEM((20 * feat, wide), BF16),
        *pair(3 * wide, outs),
        *pair(wide, outs + 4),
        keep(10 * feat, outs + 4, F32),
        plain,
        plain, *pair(feat, window), plain, plain,
        *pair(feat, window), plain, plain, plain, plain,
        *pair(feat, window),
        *pair(feat, window), plain,
        *pair(feat, window), *pair(feat, window),
        *pair(3 * feat, 3 * rows),
        keep(feat, outs, F32), *pair(4 * feat, outs), plain,
    ]
    whole = pl.BlockSpec(memory_space=pltpu.VMEM)
    grain = 8 * lax.axis_size(REDUCE_AXES)
    return pl.pallas_call(
        functools.partial(step_kernel, rows),
        out_shape=jax.ShapeDtypeStruct((-(-15 * feat // grain) * grain, wide), F32),
        in_specs=[whole] * 9,
        out_specs=whole,
        scratch_shapes=scratch,
        compiler_params=pltpu.CompilerParams(vmem_limit_bytes=60 * 1024 * 1024),
    )(vr, vf, ro, mask, rgb_weight.T, wf, wt, w2, skip_weight)


def halo_kernel(widths, count, inner, *refs):
    number = len(widths)
    fields, wholes = refs[:number], refs[number : 2 * number]
    sends, arrivals = refs[2 * number], refs[2 * number + 1]
    position = lax.axis_index("band") * inner + lax.axis_index("col")

    def device(place):
        return {"band": place // inner, "col": lax.rem(place, inner)}

    after = device(lax.rem(position + 1, count))
    before = device(lax.rem(position + count - 1, count))
    barrier = pltpu.get_barrier_semaphore()
    for peer in (after, before):
        pl.semaphore_signal(
            barrier, inc=1, device_id=peer, device_id_type=pl.DeviceIdType.MESH
        )
    pl.semaphore_wait(barrier, 2)
    copies = []
    for k in range(number):
        width, size = widths[k], fields[k].shape[0]
        moves = ((size - width, 0, after), (0, size + width, before))
        for side, (source, target, peer) in enumerate(moves):
            copies.append(
                pltpu.make_async_remote_copy(
                    src_ref=fields[k].at[pl.ds(source, width)],
                    dst_ref=wholes[k].at[pl.ds(target, width)],
                    send_sem=sends.at[2 * k + side],
                    recv_sem=arrivals.at[2 * k + side],
                    device_id=peer,
                    device_id_type=pl.DeviceIdType.MESH,
                )
            )
    for copy in copies:
        copy.start()
    for k in range(number):
        width, size = widths[k], fields[k].shape[0]
        wholes[k][width : width + size] = fields[k][...]
    for copy in copies:
        copy.wait()


def neighbours(fields, widths):
    inner = lax.axis_size("col")
    count = lax.axis_size("band") * inner
    whole = pl.BlockSpec(memory_space=pltpu.VMEM)
    number = len(fields)
    return pl.pallas_call(
        functools.partial(halo_kernel, widths, count, inner),
        out_shape=[
            jax.ShapeDtypeStruct((x.shape[0] + 2 * w,) + x.shape[1:], F32)
            for x, w in zip(fields, widths)
        ],
        in_specs=[whole] * number,
        out_specs=[whole] * number,
        scratch_shapes=[pltpu.SemaphoreType.DMA((2 * number,))] * 2,
        compiler_params=pltpu.CompilerParams(collective_id=1, has_side_effects=True),
    )(*fields)


def unpack(total, feat):
    second = total[: 9 * feat].reshape(3, 3, feat, total.shape[1])
    skip = total[9 * feat : 10 * feat]
    pairs = total[10 * feat : 13 * feat].reshape(3, feat, 2, feat)
    low = total[13 * feat : 14 * feat]
    high = total[14 * feat : 15 * feat]
    third = jnp.stack([low[:, :feat], low[:, feat:], high[:, :feat]])
    grad_first = jnp.stack([pairs[:, :, 0], pairs[:, :, 1], third], 1)
    return high[:, feat : feat + 3].T, grad_first, second, skip


def body(real_images, tile_images, rgb_weight, first_weight, second_weight, skip_weight, readout):
    row_count = real_images.shape[1]
    axes = ("band", "col")
    total_rows = row_count * lax.axis_size(axes)
    generated = lax.all_to_all(tile_images, "col", split_axis=1, concat_axis=3, tiled=True)
    vr, vf, ro = neighbours((real_images[0], generated[0], readout), (4, 2, 2))
    rows = lax.axis_index(axes) * row_count - 4 + jnp.arange(row_count + 8)
    inside = ((rows >= 0) & (rows < total_rows)).astype(F32)
    mask = jnp.broadcast_to(inside[:, None], (row_count + 8, real_images.shape[3]))
    packed = local_step(vr, vf, ro, mask, rgb_weight, first_weight, second_weight, skip_weight)
    return unpack(reduce_all(packed), skip_weight.shape[0])


def solution(mesh):
    placed = (
        P(("groups", "img"), ("band", "col"), None, None),
        P(("groups", "img"), "band", None, "col"),
        P(),
        P(),
        P(),
        P(),
        P(("band", "col"), None, None),
    )
    return jax.shard_map(
        body,
        mesh=mesh,
        in_specs=placed,
        out_specs=(
            P("groups", None),
            P("groups", None, None, None),
            P("groups", None, None, None),
            P("groups", None),
        ),
        check_vma=False,
    )
```
